32 devices in a mesh: section: 4 (over z), tm: 8 (over y, x, core).
Axes of the slice: x: 2, y: 2, z: 4, core: 2. Of those that a mesh axis runs over, the one named last changes fastest.
Arguments:
- acts_in: bfloat16 [4, 1024, 2048], P('section', 'tm'), may hold values from -6 to 6
- saved_in: bfloat16 [4, 1024, 2048], P('section', 'tm'), may hold values from -6 to 6
- grad_in: bfloat16 [4, 1024, 2048], P('section', 'tm'), may hold values from -6 to 6
- gate_a: bfloat16 [4, 2, 8, 256, 256], P('section', None, None, 'tm'), may hold values from -0.375 to 0.375
- gate_x: bfloat16 [4, 2, 8, 256, 256], P('section', None, None, 'tm'), may hold values from -0.375 to 0.375
- bias_a: float32 [4, 2, 2048], P('section'), may hold values from -4 to 4
- bias_x: float32 [4, 2, 2048], P('section'), may hold values from -4 to 4
- rate_param: float32 [4, 2, 2048], P('section'), may hold values from -16 to -3.5, as said below
- norm_gain: float32 [4, 2, 2048], P('section'), may hold values from 0.5 to 1.5
- section_layers: int32 [4], P('section'), may hold values from 1 to 2
Outputs:
- acts_out: bfloat16 [4, 1024, 2048], P('section', 'tm')
- grad_out: bfloat16 [4, 1024, 2048], P('section', 'tm')
- grad_gain: float32 [4, 2, 2048], P('section')
- grad_bias_a: float32 [4, 2, 2048], P('section')
- grad_bias_x: float32 [4, 2, 2048], P('section')
- grad_rate: float32 [4, 2, 2048], P('section')
The draws below stay inside these ranges and needn't reach their ends.
Inputs may be any that keep to these rules, and one draw needn't show every extreme that they name: `rate_param`: softplus of every entry lies between 0.05 / 1024 and 0.02.
All inputs are finite; a program needn't handle non-finite values.
Results may differ from the reference program's by a relative error of at most 0.015.
Values may be sent and summed in bfloat16 or wider, within the bound.
No kernel may reach another device: no remote copies, remote signals or barrier semaphores. Data moves between devices by JAX's collectives and lax.ppermute only.
A program may use at most 192 MiB of HBM per device.

```python
import math
import jax
import jax.numpy as jnp
from jax import lax

HEADS = 8
HW = 256
LSLOT = 2
C = 2048
SEQ = 1024
SECTIONS = 4


def draw_rate_param(key, part):
    base = jax.random.fold_in(key, 11)
    key_pick, key_slow, key_quick = jax.random.split(base, 3)
    shape = (SECTIONS, LSLOT, C)
    quick_share = 0.5
    picked = jax.random.uniform(key_pick, shape, dtype=jnp.float32) < quick_share
    slow_rate = jnp.exp(jax.random.uniform(key_slow, shape, dtype=jnp.float32, minval=math.log(0.05 / SEQ), maxval=math.log(0.2 / SEQ)))
    quick_rate = jnp.exp(jax.random.uniform(key_quick, shape, dtype=jnp.float32, minval=math.log(0.004), maxval=math.log(0.02)))
    decay_rate = jnp.where(picked, quick_rate, slow_rate)
    return jnp.log(jnp.expm1(decay_rate)).astype(jnp.float32)


def set_ends(drawn, stream_key, low, top_value):
    dims = drawn.shape
    index_at = [jax.random.randint(jax.random.fold_in(stream_key, axis), (), 0, dims[axis]) for axis in range(len(dims))]
    drawn = drawn.at[tuple(index_at)].set(low)
    longest = dims.index(max(dims))
    index_at[longest] = (index_at[longest] + 1) % dims[longest]
    return drawn.at[tuple(index_at)].set(top_value)


def levels(own_key, shape, pieces, low, high):
    factor_of, own = 1.0, jax.random.fold_in(own_key, 6)
    for axis_at, blocks in pieces:
        draws = jnp.exp(jax.random.uniform(jax.random.fold_in(own, axis_at), (blocks,), jnp.float32, low / len(pieces), high / len(pieces)))
        factor_of = factor_of * jnp.repeat(draws, shape[axis_at] // blocks).reshape([-1 if axis == axis_at else 1 for axis in range(len(shape))])
    return factor_of


def normal_values(stream_key, dims, scale, most, shards=(), kind=jnp.bfloat16):
    values = scale * jax.random.normal(stream_key, dims, jnp.float32)
    if shards:
        values = values * levels(stream_key, dims, shards, -0.22, 0.18)
    return jnp.clip(values, -most, most).astype(kind)


def setup_inputs(seed: int = 0) -> dict:
    streams_of = jax.random.split(jax.random.key(seed), 11)
    return {
        "acts_in": normal_values(streams_of[0], (SECTIONS, SEQ, C), 1.0, 6.0, ((0, 4), (1, 8))),
        "saved_in": normal_values(streams_of[1], (SECTIONS, SEQ, C), 1.0, 6.0, ((0, 4), (1, 8))),
        "grad_in": normal_values(streams_of[2], (SECTIONS, SEQ, C), 1.0, 6.0, ((0, 4), (1, 8))),
        "gate_a": normal_values(streams_of[3], (SECTIONS, LSLOT, HEADS, HW, HW), HW ** -0.5, 0.375, ((0, 4), (3, 8))),
        "gate_x": normal_values(streams_of[4], (SECTIONS, LSLOT, HEADS, HW, HW), HW ** -0.5, 0.375, ((0, 4), (3, 8))),
        "bias_a": normal_values(streams_of[5], (SECTIONS, LSLOT, C), 1.0, 4.0, ((0, 4),), jnp.float32),
        "bias_x": normal_values(streams_of[6], (SECTIONS, LSLOT, C), 1.0, 4.0, ((0, 4),), jnp.float32),
        "rate_param": draw_rate_param(jax.random.fold_in(streams_of[10], 71), 0),
        "norm_gain": jnp.clip(1.0 + 0.1 * jax.random.normal(streams_of[8], (SECTIONS, LSLOT, C), jnp.float32), 0.5, 1.5),
        "section_layers": set_ends(jax.random.randint(streams_of[9], (SECTIONS,), 1, LSLOT + 1), jax.random.fold_in(streams_of[9], 1), 1, LSLOT).astype(jnp.int32),
    }


EPS = 1e-06

def combine(earlier, later):
    return (earlier[0] * later[0], later[0] * earlier[1] + later[1])

def blockdiag(inputs, weight):
    rows_all = inputs.shape[0]
    inputs3 = inputs.astype(jnp.float32).reshape(rows_all, HEADS, HW)
    result = jnp.einsum('thi,hio->tho', inputs3, weight.astype(jnp.float32))
    return result.reshape(rows_all, HEADS * HW)

def blockdiag_t(grads, weight):
    rows_all = grads.shape[0]
    grads3 = grads.astype(jnp.float32).reshape(rows_all, HEADS, HW)
    result = jnp.einsum('tho,hio->thi', grads3, weight.astype(jnp.float32))
    return result.reshape(rows_all, HEADS * HW)

def layer_forward(x_in, w_a, w_x, b_a, b_x, rate_p, gain, live_mask):
    x_float = x_in.astype(jnp.float32)
    mean_sq = lax.optimization_barrier(jnp.mean(x_float * x_float, axis=-1, keepdims=True))
    inv_rms = lax.rsqrt(mean_sq + EPS)
    normed = x_float * inv_rms
    normed_in = (normed * gain).astype(jnp.bfloat16)
    u_float = normed_in.astype(jnp.float32)
    pre_a = blockdiag(normed_in, w_a) + b_a
    pre_x = blockdiag(normed_in, w_x) + b_x
    reset_gate = jax.nn.sigmoid(pre_a)
    input_gate = jax.nn.sigmoid(pre_x)
    decay_rate = jax.nn.softplus(rate_p)
    log_decay = -8.0 * reset_gate * decay_rate
    decay = jnp.exp(log_decay)
    scaling = jnp.sqrt(-jnp.expm1(2.0 * log_decay))
    update = scaling * input_gate * u_float
    _, states = lax.associative_scan(combine, (decay, update), axis=0)
    output = (x_float + live_mask * states).astype(jnp.bfloat16)
    return (output, (normed, inv_rms, u_float, reset_gate, input_gate, decay, scaling, states, decay_rate))

def layer_backward(upstream, stashed, w_a, w_x, rate_p, gain, live_mask):
    normed, inv_rms, u_float, reset_gate, input_gate, decay, scaling, states, decay_rate = stashed
    d_state = live_mask * upstream
    tail_a, tail_z = lax.associative_scan(combine, (decay, decay * d_state), reverse=True, axis=0)
    z_next = jnp.concatenate([tail_z[1:], jnp.zeros_like(tail_z[:1])], axis=0)
    adjoint = d_state + z_next
    h_prev = jnp.concatenate([jnp.zeros_like(states[:1]), states[:-1]], axis=0)
    d_decay = adjoint * h_prev
    d_input = adjoint * scaling * u_float
    d_log = d_decay * decay - adjoint * input_gate * u_float * decay * decay / scaling
    d_pre_a = d_log * (-8.0 * decay_rate) * reset_gate * (1.0 - reset_gate)
    d_pre_x = d_input * input_gate * (1.0 - input_gate)
    g_rate = lax.optimization_barrier(jnp.sum(d_log * (-8.0 * reset_gate), axis=0)) * jax.nn.sigmoid(rate_p)
    g_bias_a = lax.optimization_barrier(jnp.sum(d_pre_a, axis=0))
    g_bias_x = lax.optimization_barrier(jnp.sum(d_pre_x, axis=0))
    d_normed_in = adjoint * scaling * input_gate
    d_normed_in = d_normed_in + blockdiag_t(d_pre_a.astype(jnp.bfloat16), w_a)
    d_normed_in = d_normed_in + blockdiag_t(d_pre_x.astype(jnp.bfloat16), w_x)
    g_gain = lax.optimization_barrier(jnp.sum(d_normed_in * normed, axis=0))
    d_normed = d_normed_in * gain
    inner = lax.optimization_barrier(jnp.mean(d_normed * normed, axis=-1, keepdims=True))
    downstream = upstream + inv_rms * (d_normed - normed * inner)
    return (downstream, (g_gain, g_bias_a, g_bias_x, g_rate))

def one_section(per_section):
    acts, saved, grads, w_a, w_x, b_a, b_x, rate_p, gain, layer_count = per_section
    current = acts
    for slot_index in range(LSLOT):
        live_mask = (slot_index < layer_count).astype(jnp.float32)
        current, _ = layer_forward(current, w_a[slot_index], w_x[slot_index], b_a[slot_index], b_x[slot_index], rate_p[slot_index], gain[slot_index], live_mask)
    forward_result = current
    recomputed = saved
    stash_list = []
    for slot_index in range(LSLOT):
        live_mask = (slot_index < layer_count).astype(jnp.float32)
        recomputed, stashed = layer_forward(recomputed, w_a[slot_index], w_x[slot_index], b_a[slot_index], b_x[slot_index], rate_p[slot_index], gain[slot_index], live_mask)
        stash_list.append(stashed)
    upstream = grads.astype(jnp.float32)
    grad_lists = [None] * LSLOT
    for slot_index in reversed(range(LSLOT)):
        live_mask = (slot_index < layer_count).astype(jnp.float32)
        upstream, slot_grads = layer_backward(upstream, stash_list[slot_index], w_a[slot_index], w_x[slot_index], rate_p[slot_index], gain[slot_index], live_mask)
        grad_lists[slot_index] = slot_grads
    stacked = tuple((jnp.stack([grad_lists[k][m] for k in range(LSLOT)], axis=0) for m in range(4)))
    return (forward_result, upstream.astype(jnp.bfloat16)) + stacked

def reference(acts_in, saved_in, grad_in, gate_a, gate_x, bias_a, bias_x, rate_param, norm_gain, section_layers):
    results = lax.map(one_section, (acts_in, saved_in, grad_in, gate_a, gate_x, bias_a, bias_x, rate_param, norm_gain, section_layers))
    forward_all, downstream_all, g_gain, g_bias_a, g_bias_x, g_rate = results
    acts_out = jnp.roll(forward_all, 1, axis=0)
    grad_out = jnp.roll(downstream_all, -1, axis=0)
    return (acts_out, grad_out, g_gain, g_bias_a, g_bias_x, g_rate)
```

```python
import functools

import jax
import jax.numpy as jnp
from jax import lax
from jax.experimental import pallas as pl
from jax.experimental.pallas import tpu as pltpu
from jax.sharding import PartitionSpec as P

EPS = 1e-06
SEG = 8
F32 = jnp.float32
BF16 = jnp.bfloat16
MOST_DIRECT = 8
ROWS = 32


def flip(value, axis, bit):
    count = lax.axis_size(axis)
    return lax.ppermute(value, axis, [(source, source ^ bit) for source in range(count)])


def is_direct(count):
    return count <= MOST_DIRECT and count & (count - 1) == 0


def relay_gather(value, axis, order):
    pieces = {0: value}
    for bit in order:
        pieces.update({k | bit: flip(part, axis, bit) for k, part in list(pieces.items())})
    return [pieces[k] for k in sorted(pieces)]


def small_gather(value, axis):
    count = lax.axis_size(axis)
    if not is_direct(count):
        return [lax.all_gather(value, axis)]
    pieces = {0: value}
    for k in reversed(range(2, count, 2)):
        pieces[k] = flip(value, axis, k)
    for k in range(0, count, 2):
        if k + 1 < count:
            pieces[k + 1] = flip(pieces[k], axis, 1)
    return [pieces[k] for k in sorted(pieces)]


def weight_gather(value, axis, first_low):
    count = lax.axis_size(axis)
    if not is_direct(count):
        return [lax.all_gather(value, axis, axis=1, tiled=True)]
    bits = [1 << b for b in range(count.bit_length() - 1)]
    far = bits[1:] if first_low else bits[:0:-1]
    return relay_gather(value, axis, far + bits[:1])


def from_behind(value, axis, steps):
    count = lax.axis_size(axis)
    pairs = [(source, (source + steps) % count) for source in range(count)]
    return lax.ppermute(value, axis, pairs)


def vmem(shape, dtype):
    return pltpu.VMEM(shape, dtype)


def run(body, outs, args, scratch=(), smem=0, flops=0, name=None):
    specs = [pl.BlockSpec(memory_space=pltpu.SMEM)] * smem
    specs += [pl.BlockSpec(memory_space=pltpu.VMEM)] * (len(args) - smem)
    moved = sum(a.size * a.dtype.itemsize for a in args)
    return pl.pallas_call(
        body,
        out_shape=outs,
        in_specs=specs,
        out_specs=[pl.BlockSpec(memory_space=pltpu.VMEM)] * len(outs),
        scratch_shapes=list(scratch),
        compiler_params=pltpu.CompilerParams(vmem_limit_bytes=20 * 1024 * 1024),
        cost_estimate=pl.CostEstimate(flops=flops, bytes_accessed=moved, transcendentals=0),
        name=name,
    )(*args)


def order_matrix(rows, inverse):
    steps = rows // SEG
    first = lax.broadcasted_iota(jnp.int32, (rows, rows), 1 if inverse else 0)
    second = lax.broadcasted_iota(jnp.int32, (rows, rows), 0 if inverse else 1)
    return ((first % SEG) * steps + first // SEG == second).astype(F32).astype(BF16)


def lanes(head, width):
    return pl.ds(pl.multiple_of(head * width, width), width)


def sigmoid(value):
    return pl.reciprocal(1.0 + jnp.exp(jnp.minimum(-value, 87.0)))


def expm1_small(v):
    s = 1.0 / 720.0 + v * (1.0 / 5040.0)
    s = 1.0 / 120.0 + v * s
    s = 1.0 / 24.0 + v * s
    s = 1.0 / 6.0 + v * s
    s = 0.5 + v * s
    return v + v * (v * s)


def place_pieces(mine, pieces, full_ref, axis_rows):
    if len(pieces) == 1:
        full_ref[...] = pieces[0][...]
        return
    for k, piece in enumerate(pieces):
        start = pl.multiple_of((mine ^ k) * axis_rows, axis_rows)
        full_ref[:, pl.ds(start, axis_rows), :] = piece[...]


def place_small(mine, pieces, full_ref):
    if len(pieces) == 1:
        full_ref[...] = pieces[0][...]
        return
    for k, piece in enumerate(pieces):
        full_ref[mine ^ k] = piece[...]


def carry_from_left(all_ref, mine, count, at_a, at_b, heads):
    carry = jnp.zeros((heads, all_ref.shape[2]), F32)
    for k in range(count - 1):
        a = all_ref[k, at_a * heads : (at_a + 1) * heads, :]
        b = all_ref[k, at_b * heads : (at_b + 1) * heads, :]
        carry = jnp.where(k < mine, a * carry + b, carry)
    return carry


def carry_from_right(a_of, z_of, mine, count, heads, width):
    carry = jnp.zeros((heads, width), F32)
    for k in reversed(range(1, count)):
        carry = jnp.where(k > mine, a_of(k) * carry + z_of(k), carry)
    return carry


def prefix_rows(total_a, total_b, reverse):
    width = total_a.shape[1]
    run_a, run_b = jnp.ones((1, width), F32), jnp.zeros((1, width), F32)
    in_a, in_b = [None] * SEG, [None] * SEG
    for s in reversed(range(SEG)) if reverse else range(SEG):
        in_a[s], in_b[s] = run_a, run_b
        a, b = total_a[s : s + 1], total_b[s : s + 1]
        run_b = a * run_b + b
        run_a = a * run_a
    return jnp.concatenate(in_a, 0), jnp.concatenate(in_b, 0), run_a, run_b


def entry_kernel(acts, saved, grad, gain, xa, ua, xs, us, inv_s, gp):
    rows, channels = acts.shape
    order = order_matrix(rows, False)
    for src, x_out, u_out, inv_out in ((saved, xs, us, inv_s), (acts, xa, ua, None)):
        x = jnp.dot(order, src[...], preferred_element_type=F32)
        x_out[...] = x.astype(BF16)
        inv = lax.rsqrt(jnp.mean(x * x, axis=-1, keepdims=True) + EPS)
        u_out[...] = ((x * inv) * gain[...]).astype(BF16)
        if inv_out is not None:
            inv_out[...] = jnp.broadcast_to(inv, inv_out.shape)
    gp[...] = jnp.dot(order, grad[...], preferred_element_type=F32).astype(BF16)


def gates_and_scan(u_ref, wa, wx, ba, bx, n8r, head, width, local, keep, reverse_of):
    at = lanes(head, width)
    hl, ac, pre_b, pre_a, pay, pay_a, pay_b = local
    rows, heads = u_ref.shape[0], wa.shape[0]
    u_h = u_ref[:, at]
    full_a = jnp.dot(u_h, wa[head], preferred_element_type=F32)
    full_x = jnp.dot(u_h, wx[head], preferred_element_type=F32)
    bias_a, bias_x, rate = ba[:, at], bx[:, at], n8r[:, at]
    run_a = jnp.ones((SEG, width), F32)
    run_h = jnp.zeros((SEG, width), F32)
    chunk = min(ROWS, rows)
    for c in range(0, rows, chunk):
        block = slice(c, c + chunk)
        r = sigmoid(full_a[block] + bias_a)
        i = sigmoid(full_x[block] + bias_x)
        e = expm1_small(r * rate)
        a = 1.0 + e
        square = -e * (2.0 + e)
        inv_scale = lax.rsqrt(jnp.maximum(square, 1e-37))
        scale = square * inv_scale
        b = scale * i * u_h[block].astype(F32)
        if keep is not None:
            for ref, value in zip(keep, (r, i, a, scale, inv_scale)):
                ref[block, at] = value
        for j in range(0, chunk, SEG):
            a_j = a[j : j + SEG]
            run_h = a_j * run_h + b[j : j + SEG]
            run_a = a_j * run_a
            hl[c + j : c + j + SEG, at] = run_h
            ac[c + j : c + j + SEG, at] = run_a
    in_a, in_b, tot_a, tot_b = prefix_rows(run_a, run_h, False)
    pre_a[:, at] = in_a
    pre_b[:, at] = in_b
    pay[pl.ds(pay_a * heads + head, 1), :] = tot_a
    pay[pl.ds(pay_b * heads + head, 1), :] = tot_b
    if reverse_of is not None:
        dy_of, a_ref, live, rev, pay_z = reverse_of
        reverse_scan(dy_of, a_ref, live, at, rev, pay, pay_z * heads + head)


def reverse_scan(dy_of, a_ref, live, at, rev, pay, row):
    ql, aq, suf_a, suf_b = rev
    rows = a_ref.shape[0]
    width = ql.shape[1] // (ql.shape[1] // at.size)
    run_a = jnp.ones((SEG, width), F32)
    run_z = jnp.zeros((SEG, width), F32)
    for j in reversed(range(0, rows, SEG)):
        block = slice(j, j + SEG)
        q = live * dy_of(block, at) + run_z
        ql[block, at] = q
        aq[block, at] = run_a
        a_j = a_ref[block, at]
        run_z = a_j * q
        run_a = a_j * run_a
    in_a, in_b, _, tot_b = prefix_rows(run_a, run_z, True)
    suf_a[:, at] = in_a
    suf_b[:, at] = in_b
    if pay is not None:
        pay[pl.ds(row, 1), :] = tot_b


def forward_kernel(count, first, last, n_w, n_s, heads, width, names, *refs):
    r = dict(zip(names, refs))
    mine = r["mine"][0]
    wa, wx = r["wa"], r["wx"]
    piece_rows = r["pa0"].shape[1]
    place_pieces(mine, [r[f"pa{k}"] for k in range(n_w)], wa, piece_rows)
    place_pieces(mine, [r[f"px{k}"] for k in range(n_w)], wx, piece_rows)
    if not first:
        live = r["live"][0]
        got = r["got"]
        place_small(mine, [r[f"s{k}"] for k in range(n_s)], got)
        rows, channels = r["x_s"].shape
        for stream in ("s", "a"):
            where_a, where_b = (0, 1) if stream == "s" else (2, 3)
            r["carry"][...] = carry_from_left(got, mine, count, where_a, where_b, heads)
            squares = r["squares"]
            squares[...] = jnp.zeros_like(squares)

            def apply(head, _, stream=stream, squares=squares):
                at = lanes(head, width)
                enter = r["pb_" + stream][:, at] + r["pa_" + stream][:, at] * r["carry"][pl.ds(head, 1), :]
                if stream == "s":
                    r["enter_s"][:, at] = enter
                for j in range(0, rows, SEG):
                    block = slice(j, j + SEG)
                    h = r["hl_" + stream][block, at] + r["ac_" + stream][block, at] * enter
                    y = r["x_" + stream][block, at].astype(F32) + live * h
                    y = y.astype(BF16)
                    r["y_" + stream][block, at] = y
                    y = y.astype(F32)
                    squares[block, :] += y * y
                return _

            lax.fori_loop(0, heads, apply, 0)
            inv = lax.rsqrt(jnp.sum(squares[...], axis=-1, keepdims=True) / channels + EPS)
            r["inv"][...] = jnp.broadcast_to(inv, r["inv"].shape)
            if stream == "s":
                r["inv_s"][...] = jnp.broadcast_to(inv, r["inv_s"].shape)

            def norm(head, _, stream=stream):
                at = lanes(head, width)
                y = r["y_" + stream][:, at].astype(F32)
                r["u_" + stream][:, at] = ((y * r["inv"][:, :1]) * r["gain"][:, at]).astype(BF16)
                return _

            lax.fori_loop(0, heads, norm, 0)
    pay = r["pay"]
    keep = [r["k" + k] for k in "riasv"]
    rev = None
    if last:
        g = r["gp"]
        live_next = r["live"][1]
        rev = (
            lambda block, at: g[block, at].astype(F32),
            r["ka"],
            live_next,
            (r["ql"], r["aq"], r["sa"], r["sb"]),
            4,
        )

    def one(head, _):
        for stream in ("s", "a"):
            t = "n" + stream
            local = (r["hl_" + t], r["ac_" + t], r["pb_" + t], r["pa_" + t], pay)
            local += (0, 1) if stream == "s" else (2, 3)
            gates_and_scan(
                r["u_" + stream], wa, wx, r["ba"], r["bx"], r["n8r"], head, width, local,
                keep if stream == "s" else None, rev if stream == "s" else None,
            )
        return _

    lax.fori_loop(0, heads, one, 0)


def acts_kernel(count, n_s, heads, width, names, *refs):
    r = dict(zip(names, refs))
    mine, live = r["mine"][0], r["live"][1]
    got = r["got"]
    place_small(mine, [r[f"s{k}"] for k in range(n_s)], got)
    r["carry"][...] = carry_from_left(got, mine, count, 2, 3, heads)
    rows = r["x"].shape[0]

    def apply(head, _):
        at = lanes(head, width)
        enter = r["pb"][:, at] + r["pa"][:, at] * r["carry"][pl.ds(head, 1), :]
        for j in range(0, rows, SEG):
            block = slice(j, j + SEG)
            h = r["hl"][block, at] + r["ac"][block, at] * enter
            r["y"][block, at] = r["x"][block, at].astype(F32) + live * h
        return _

    lax.fori_loop(0, heads, apply, 0)
    back = order_matrix(rows, True)
    r["out"][...] = jnp.dot(back, r["y"][...].astype(BF16), preferred_element_type=F32).astype(BF16)


def backward_kernel(count, final, top, n_s, n_z, heads, width, names, *refs):
    r = dict(zip(names, refs))
    mine = r["mine"][0]
    got = r["got"]
    place_small(mine, [r[f"s{k}"] for k in range(n_s)], got)
    rows, channels = r["x"].shape
    if top:
        a_of = lambda k: got[k, :heads, :]
        z_of = lambda k: got[k, 4 * heads : 5 * heads, :]
        r["carry"][...] = carry_from_left(got, mine, count, 0, 1, heads)
    else:
        place_small(mine, [r[f"z{k}"] for k in range(n_z)], r["gotz"])
        a_of = lambda k: got[k, :heads, :]
        z_of = lambda k: r["gotz"][k]
    r["carry_z"][...] = carry_from_right(a_of, z_of, mine, count, heads, width)
    cross = r["cross"]
    cross[...] = jnp.zeros_like(cross)
    du_ref, sums = r["du"], r["sums"]
    chunk = min(ROWS, rows)
    contract = (((1,), (1,)), ((), ()))

    def one(head, _):
        at = lanes(head, width)
        if top:
            enter = r["pb"][:, at] + r["pa"][:, at] * r["carry"][pl.ds(head, 1), :]
        else:
            enter = r["enter"][:, at]
        enter_z = r["sb"][:, at] + r["sa"][:, at] * r["carry_z"][pl.ds(head, 1), :]
        tile = lambda v, n: jnp.concatenate([v] * n, 0) if n > 1 else v
        n8r = r["n8r"][:, at]
        sum_m = jnp.zeros((SEG, width), F32)
        sum_a, sum_x, sum_g = sum_m, sum_m, sum_m
        last_h = enter
        fold = lambda v: sum(v[j : j + SEG] for j in range(0, v.shape[0], SEG))
        for c in range(0, rows, chunk):
            block = slice(c, c + chunk)
            n = chunk // SEG
            h = r["hl"][block, at] + r["ac"][block, at] * tile(enter, n)
            h_prev = jnp.concatenate([last_h, h[:-SEG]], 0) if n > 1 else last_h
            last_h = h[-SEG:]
            q = r["ql"][block, at] + r["aq"][block, at] * tile(enter_z, n)
            gr, gi, a = r["kr"][block, at], r["ki"][block, at], r["ka"][block, at]
            scale, inv_scale = r["ks"][block, at], r["kv"][block, at]
            u = r["u"][block, at].astype(F32)
            iu = gi * u
            qs = q * scale
            m = q * a * (h_prev - iu * a * inv_scale) * gr
            d_a = m * (1.0 - gr) * n8r
            d_x = qs * iu * (1.0 - gi)
            sum_m += fold(m)
            sum_a += fold(d_a)
            sum_x += fold(d_x)
            r["da"][block, :] = d_a.astype(BF16)
            r["dx"][block, :] = d_x.astype(BF16)
            du_ref[block, at] = qs * gi
        mixed = lax.dot_general(r["da"][...], r["wa"][head], contract, preferred_element_type=F32)
        mixed += lax.dot_general(r["dx"][...], r["wx"][head], contract, preferred_element_type=F32)
        gain = r["gain"][:, at]
        for c in range(0, rows, chunk):
            block = slice(c, c + chunk)
            du = du_ref[block, at] + mixed[block]
            normed = r["x"][block, at].astype(F32) * r["inv"][block, :1]
            t = du * normed
            sum_g += fold(t)
            cross[block, :] += t * gain
            du_ref[block, at] = du
        total = lambda v: jnp.sum(v, axis=0, keepdims=True)
        sums[pl.ds(head, 1), :] = total(sum_g)
        sums[pl.ds(heads + head, 1), :] = total(sum_a)
        sums[pl.ds(2 * heads + head, 1), :] = total(sum_x)
        sums[pl.ds(3 * heads + head, 1), :] = total(sum_m) * (-8.0 * r["sig"][:, at])
        return _

    lax.fori_loop(0, heads, one, 0)
    inv = r["inv"][:, :1]
    inner = jnp.sum(cross[...], axis=-1, keepdims=True) / channels
    r["c1"][...] = jnp.broadcast_to(inv * inv * inner, r["c1"].shape)

    def down(head, _):
        at = lanes(head, width)
        for c in range(0, rows, chunk):
            block = slice(c, c + chunk)
            dn = du_ref[block, at] * r["gain"][:, at]
            x = r["x"][block, at].astype(F32)
            dy = r["dy"][block, at].astype(F32)
            r["ndy"][block, at] = dy + (dn * r["inv"][block, :1] - x * r["c1"][block, :1])
        if not final:
            reverse_scan(
                lambda block, at: r["ndy"][block, at], r["ka_lo"], r["live_lo"][0], at,
                (r["nql"], r["naq"], r["nsa"], r["nsb"]), r["pay"], head,
            )
        return _

    lax.fori_loop(0, heads, down, 0)
    if final:
        back = order_matrix(rows, True)
        r["out"][...] = jnp.dot(back, r["ndy"][...].astype(BF16), preferred_element_type=F32).astype(BF16)


def sum_kernel(n_s, slots, heads, width, names, *refs):
    r = dict(zip(names, refs))
    pieces = [r[f"s{k}"] for k in range(n_s)]
    if n_s == 1:
        total = jnp.sum(pieces[0][...].astype(F32), axis=0)
    else:
        total = sum(piece[...].astype(F32) for piece in pieces)
    for slot in range(slots):
        for kind in range(4):
            for head in range(heads):
                row = (slot * 4 + kind) * heads + head
                r[f"g{kind}"][slot : slot + 1, head * width : (head + 1) * width] = total[row : row + 1]


def named_run(body, ins, outs, scratch, smem, name):
    names = list(ins) + list(outs) + list(scratch)
    result = run(
        functools.partial(body, names), list(outs.values()), list(ins.values()),
        list(scratch.values()), smem, name=name,
    )
    return dict(zip(outs, result))


def local(
    acts_in, saved_in, grad_in, gate_a, gate_x, bias_a, bias_x, rate_param, norm_gain, section_layers
):
    rows, channels = acts_in.shape[1:]
    slots, heads, piece_rows, width = gate_a.shape[1:]
    count = lax.axis_size("tm")
    mine = lax.axis_index("tm").astype(jnp.int32)[None]
    live = (jnp.arange(slots, dtype=jnp.int32) < section_layers[0]).astype(F32)
    n8r = -8.0 * jax.nn.softplus(rate_param[0])
    sig = jax.nn.sigmoid(rate_param[0])
    big, row8, lane_stat = (rows, channels), (SEG, channels), (rows, 128)

    weights = [
        (
            weight_gather(gate_a[0, slot], "tm", True),
            weight_gather(gate_x[0, slot], "tm", False),
        )
        for slot in range(slots)
    ]
    row_of = lambda array, slot: array[slot : slot + 1]
    xa, ua, xs, us, inv, gp = run(
        entry_kernel,
        [vmem(big, BF16)] * 4 + [vmem(lane_stat, F32), vmem(big, BF16)],
        [acts_in[0], saved_in[0], grad_in[0], row_of(norm_gain[0], 0)],
        name="entry",
    )
    stash, now, got = [], {"x_s": xs, "x_a": xa, "u_s": us, "u_a": ua, "inv_s": inv}, None
    before = None
    for slot in range(slots):
        first, last = slot == 0, slot == slots - 1
        parts = 5 if last else 4
        ins = {"mine": mine}
        smem = 1
        if not first or last:
            lo = max(slot - 1, 0)
            ins["live"] = live[lo : lo + 2] if not first else jnp.concatenate([live[:1], live[:1]])
            smem = 2
        pieces_a, pieces_x = weights[slot]
        ins.update({f"pa{k}": piece for k, piece in enumerate(pieces_a)})
        ins.update({f"px{k}": piece for k, piece in enumerate(pieces_x)})
        ins.update(ba=row_of(bias_a[0], slot), bx=row_of(bias_x[0], slot), n8r=row_of(n8r, slot))
        outs = {"wa": vmem((heads, width, width), BF16), "wx": vmem((heads, width, width), BF16)}
        outs["pay"] = vmem((parts * heads, width), F32)
        scratch = {}
        if first:
            ins.update(u_s=now["u_s"], u_a=now["u_a"])
        else:
            ins.update({f"s{k}": piece for k, piece in enumerate(got)})
            ins["gain"] = row_of(norm_gain[0], slot)
            for stream in "sa":
                ins["x_" + stream] = now["x_" + stream]
                for kind in ("hl_", "ac_", "pa_", "pb_"):
                    ins[kind + stream] = before[kind + "n" + stream]
                outs["y_" + stream] = vmem(big, BF16)
            outs["u_s"] = vmem(big, BF16)
            outs["enter_s"] = vmem(row8, F32)
            outs["inv_s"] = vmem(lane_stat, F32)
            scratch.update(
                u_a=pltpu.VMEM(big, BF16),
                got=pltpu.VMEM((count, 4 * heads, width), F32),
                carry=pltpu.VMEM((heads, width), F32),
                squares=pltpu.VMEM((rows, width), F32),
                inv=pltpu.VMEM(lane_stat, F32),
            )
        if last:
            ins["gp"] = gp
            for kind in ("ql", "aq"):
                outs[kind] = vmem(big, F32)
            for kind in ("sa", "sb"):
                outs[kind] = vmem(row8, F32)
        for stream in "sa":
            for kind in ("hl_n", "ac_n"):
                outs[kind + stream] = vmem(big, F32)
            for kind in ("pa_n", "pb_n"):
                outs[kind + stream] = vmem(row8, F32)
        for kind in "riasv":
            outs["k" + kind] = vmem(big, F32)
        body = functools.partial(
            forward_kernel, count, first, last, len(pieces_a), 0 if first else len(got), heads, width
        )
        out = named_run(body, ins, outs, scratch, smem, f"forward{slot}")
        if not first:
            now = {
                "x_s": out["y_s"], "x_a": out["y_a"], "u_s": out["u_s"], "inv_s": out["inv_s"],
            }
            stash[-1]["enter"] = out["enter_s"]
        kept = {"k" + kind: out["k" + kind] for kind in "riasv"}
        kept.update(x=now["x_s"], u=now["u_s"], inv=now["inv_s"], wa=out["wa"], wx=out["wx"])
        kept.update(hl=out["hl_ns"], ac=out["ac_ns"], pa=out["pa_ns"], pb=out["pb_ns"])
        got = small_gather(out["pay"], "tm")
        kept["got"] = got
        stash.append(kept)
        before = out

    ins = {"mine": mine, "live": jnp.concatenate([live[-1:], live[-1:]])}
    ins.update({f"s{k}": piece for k, piece in enumerate(got)})
    ins.update(x=now["x_a"], hl=before["hl_na"], ac=before["ac_na"], pa=before["pa_na"], pb=before["pb_na"])
    forwarded = named_run(
        functools.partial(acts_kernel, count, len(got), heads, width),
        ins,
        {"out": jax.ShapeDtypeStruct(big, BF16)},
        {
            "got": pltpu.VMEM((count, 5 * heads, width), F32),
            "carry": pltpu.VMEM((heads, width), F32),
            "y": pltpu.VMEM(big, F32),
        },
        2,
        "acts",
    )["out"]
    acts_out = from_behind(forwarded[None], "section", 1)

    dy = gp
    reverse = {kind: before[kind] for kind in ("ql", "aq", "sa", "sb")}
    got_z = None
    sums = [None] * slots
    for slot in reversed(range(slots)):
        top, final = slot == slots - 1, slot == 0
        kept = stash[slot]
        ins = {"mine": mine}
        smem = 1
        if not final:
            ins["live_lo"] = live[slot - 1 : slot]
            smem = 2
        ins.update({f"s{k}": piece for k, piece in enumerate(kept["got"])})
        if not top:
            ins.update({f"z{k}": piece for k, piece in enumerate(got_z)})
            ins["enter"] = kept["enter"]
        else:
            ins.update(pa=kept["pa"], pb=kept["pb"])
        for kind in ("x", "u", "inv", "wa", "wx", "hl", "ac", "kr", "ki", "ka", "ks", "kv"):
            ins[kind] = kept[kind]
        ins.update(reverse)
        ins.update(dy=dy, gain=row_of(norm_gain[0], slot), n8r=row_of(n8r, slot), sig=row_of(sig, slot))
        outs = {"sums": vmem((4 * heads, width), F32)}
        scratch = {
            "got": pltpu.VMEM((count, (5 if top else 4) * heads, width), F32),
            "carry_z": pltpu.VMEM((heads, width), F32),
            "carry": pltpu.VMEM((heads, width), F32),
            "cross": pltpu.VMEM((rows, width), F32),
            "du": pltpu.VMEM(big, F32),
            "da": pltpu.VMEM((rows, width), BF16),
            "dx": pltpu.VMEM((rows, width), BF16),
            "c1": pltpu.VMEM(lane_stat, F32),
        }
        if not top:
            scratch["gotz"] = pltpu.VMEM((count, heads, width), F32)
        if final:
            outs["out"] = jax.ShapeDtypeStruct(big, BF16)
            scratch["ndy"] = pltpu.VMEM(big, F32)
        else:
            ins["ka_lo"] = stash[slot - 1]["ka"]
            outs.update(ndy=vmem(big, F32), nql=vmem(big, F32), naq=vmem(big, F32))
            outs.update(nsa=vmem(row8, F32), nsb=vmem(row8, F32), pay=vmem((heads, width), F32))
        body = functools.partial(
            backward_kernel, count, final, top, len(kept["got"]), 0 if top else len(got_z), heads, width
        )
        out = named_run(body, ins, outs, scratch, smem, f"backward{slot}")
        sums[slot] = out["sums"]
        if not final:
            dy = out["ndy"]
            reverse = {kind: out["n" + kind] for kind in ("ql", "aq", "sa", "sb")}
            got_z = small_gather(out["pay"], "tm")
    grad_out = from_behind(out["out"][None], "section", -1)
    pieces = small_gather(jnp.concatenate(sums, 0).astype(BF16), "tm")
    grads = named_run(
        functools.partial(sum_kernel, len(pieces), slots, heads, width),
        {f"s{k}": piece for k, piece in enumerate(pieces)},
        {f"g{kind}": jax.ShapeDtypeStruct((slots, channels), F32) for kind in range(4)},
        {},
        0,
        "sums",
    )
    return (acts_out, grad_out) + tuple(grads[f"g{kind}"][None] for kind in range(4))


def solution(mesh):
    return jax.shard_map(
        local,
        mesh=mesh,
        in_specs=(
            P("section", "tm", None),
            P("section", "tm", None),
            P("section", "tm", None),
            P("section", None, None, "tm", None),
            P("section", None, None, "tm", None),
            P("section", None, None),
            P("section", None, None),
            P("section", None, None),
            P("section", None, None),
            P("section"),
        ),
        out_specs=(
            P("section", "tm", None),
            P("section", "tm", None),
            P("section", None, None),
            P("section", None, None),
            P("section", None, None),
            P("section", None, None),
        ),
        check_vma=False,
    )
```
